128 devices in a mesh: fsdp: 32 (over x, z, core), tp: 4 (over y).
Axes of the slice: x: 4, y: 4, z: 4, core: 2. Of those that a mesh axis runs over, the one named last changes fastest.
Arguments:
- grads: bfloat16 [32, 32, 768, 1280], P('fsdp', None, 'tp'), may hold values from -22 to 22
- momentum: float32 [64, 768, 1280], P('fsdp', 'tp'), may hold values from -6 to 6
- weights: float32 [32, 768, 1280], P(None, 'tp', 'fsdp'), may hold values from -6 to 6
- owners: int32 [32], replicated, may hold values from 0 to 31, as said below
- vec_grads: float32 [128, 81920], P(('fsdp', 'tp')), may hold values from -24 to 24
- vec_params: float32 [81920], P(('fsdp', 'tp')), may hold values from 0.5 to 1.5
- vec_m: float32 [81920], P(('fsdp', 'tp')), may hold values from -6 to 6
- vec_v: float32 [81920], P(('fsdp', 'tp')), may hold values from 0.5 to 500
Outputs:
- new_weights: float32 [32, 768, 1280], P(None, 'tp', 'fsdp')
- update: bfloat16 [32, 768, 1280], P(None, 'tp', 'fsdp')
- new_momentum: float32 [64, 768, 1280], P('fsdp', 'tp')
- new_vec_params: float32 [81920], P(('fsdp', 'tp'))
- new_vec_m: float32 [81920], P(('fsdp', 'tp'))
- new_vec_v: float32 [81920], P(('fsdp', 'tp'))
The draws below stay inside these ranges and needn't reach their ends.
Inputs may be any that keep to these rules, and one draw needn't show every extreme that they name: `owners`: each owner index appears at most 2 times, and some index appears exactly 2 times.
All inputs are finite; a program needn't handle non-finite values.
Results may differ from the reference program's by a relative error of at most 0.035.
Values may be sent and summed in bfloat16 or wider, within the bound.
A program may use at most 192 MiB of HBM per device.

```python
import math
import jax
import jax.numpy as jnp
from jax import lax

D = 1280
HD = 768
OWN_MAX = 2
NS_ITERS = 3
LAYERS = 32
SLOTS = 64
NVEC = 81920
N_FSDP = 32
N_TP = 4


def draw_grads(key, part):
    keys = jax.random.split(key, 4)
    positions = jnp.arange(HD).astype(jnp.float32)
    trend = jnp.exp(math.log(3.0) * positions / (HD - 1))
    row_scale = trend * jnp.exp(jax.random.uniform(keys[0], (HD,), jnp.float32, 0.0, math.log(10.0)))
    col_scale = jnp.exp(jax.random.uniform(keys[1], (D,), jnp.float32, 0.0, math.log(10.0)))
    pairing = jax.random.permutation(keys[2], N_FSDP)
    column_block = jnp.arange(D) // (D // N_FSDP)
    boost = jnp.where(column_block[None, :] == pairing[:, None], 3.0, 1.0).astype(jnp.float32)
    noise = jax.random.truncated_normal(keys[3], -6.0, 6.0, (N_FSDP, LAYERS, HD, D), jnp.float32)
    values = 0.02 * noise * row_scale[None, None, :, None] * col_scale[None, None, None, :] * boost[:, None, None, :]
    return jnp.clip(values, -22.0, 22.0).astype(jnp.bfloat16)


def draw_owners(key, part):
    keys = jax.random.split(jax.random.fold_in(key, 7), 2)
    slot_total = N_FSDP * OWN_MAX
    order_slots = jax.random.permutation(keys[0], slot_total)
    first = order_slots[0]
    partner = first // OWN_MAX * OWN_MAX + (first + 1) % OWN_MAX
    order = jnp.argsort((order_slots == partner).astype(jnp.int32), stable=True)
    rest = order_slots[order]
    chosen = jnp.concatenate([first[None], partner[None], rest[1:LAYERS - 1]])
    shuffled = jax.random.permutation(keys[1], chosen)
    return (shuffled // OWN_MAX).astype(jnp.int32)


def raised(entries, own_key, source, target, shards_of, factor):
    def block_of(axis_at):
        return (jnp.arange(entries.shape[axis_at]) // (entries.shape[axis_at] // shards_of)).reshape((-1,) + (1,) * (entries.ndim - 1 - axis_at))

    first = jax.random.permutation(own_key, shards_of)[block_of(target)]
    second = (block_of(target) + shards_of // 2) % shards_of
    return jnp.where((block_of(source) == first) | (block_of(source) == second), factor * entries, entries)


def levels(own_key, dims, pieces, smallest, largest):
    def one(dim, blocks):
        heights = jax.random.uniform(jax.random.fold_in(jax.random.fold_in(own_key, 6), dim), (blocks,), jnp.float32, smallest / len(pieces), largest / len(pieces))
        return jnp.repeat(jnp.exp(heights), dims[dim] // blocks).reshape((-1,) + (1,) * (len(dims) - dim - 1))

    loudness = one(*pieces[0])
    for cut in pieces[1:]:
        loudness = loudness * one(*cut)
    return loudness


def centred(rng, shape, spread, bound, cuts=(), held_as=jnp.bfloat16):
    array = jax.random.normal(rng, shape, jnp.float32) * spread
    if len(cuts) > 0:
        array = levels(rng, shape, cuts, -0.22, 0.18) * array
    return jnp.clip(array, min=-bound, max=bound).astype(held_as)


def gaussian_with(stream_key, shape, width, most, pieces, heavy, dtype=jnp.bfloat16):
    array = width * jax.random.normal(stream_key, shape, jnp.float32)
    if pieces:
        array = array * levels(stream_key, shape, pieces, -0.22, 0.18)
    return jnp.clip(raised(array, jax.random.fold_in(stream_key, 3), *heavy), -most, most).astype(dtype)


def setup_inputs(seed: int = 0) -> dict:
    splits = jax.random.split(jax.random.key(seed), 9)
    grads = draw_grads(jax.random.fold_in(splits[8], 71), 0)
    momentum = centred(splits[1], (SLOTS, HD, D), 2.0, 6.0, ((0, 32), (1, 4)), jnp.float32)
    weights = centred(splits[2], (LAYERS, HD, D), 0.5, 6.0, ((1, 4), (2, 32)), jnp.float32)
    owners = draw_owners(jax.random.fold_in(splits[8], 71), 0)
    vec_grads = gaussian_with(splits[4], (N_FSDP * N_TP, NVEC), 1.0, 24.0, ((0, 128),), (0, 1, 128, 5.5), jnp.float32)
    vec_params = jnp.clip(1.0 + 0.1 * jax.random.normal(splits[5], (NVEC,), jnp.float32), 0.5, 1.5)
    vec_m = centred(splits[6], (NVEC,), 0.5, 6.0, ((0, 128),), jnp.float32)
    vec_v = jnp.clip(jnp.exp(math.log(500.0) - 6.9077553 * jax.random.uniform(splits[7], (NVEC,), jnp.float32) ** levels(splits[7], (NVEC,), ((0, 128),), -0.2, 0.2)), 0.5, 500.0)
    return dict(grads=grads, momentum=momentum, weights=weights, owners=owners, vec_grads=vec_grads, vec_params=vec_params, vec_m=vec_m, vec_v=vec_v)


BETA = 0.5
EPS_NORM = 1e-07
COEF_A = 3.4445
COEF_B = -4.775
COEF_C = 2.0315
MUON_RATE = 0.02
DECAY = 0.1
VEC_RATE = 0.01
ADAM_ONE = 0.9
ADAM_TWO = 0.95
BIAS_ONE = 1.0 - 0.9 ** 10
BIAS_TWO = 1.0 - 0.95 ** 10
ADAM_EPS = 1e-08

def newton_schulz(matrix):
    for step in range(NS_ITERS):
        gram = jnp.dot(matrix, matrix.T, preferred_element_type=jnp.float32).astype(jnp.bfloat16)
        square = jnp.dot(gram, gram, preferred_element_type=jnp.float32)
        poly = (COEF_B * gram.astype(jnp.float32) + COEF_C * square).astype(jnp.bfloat16)
        matrix = (COEF_A * matrix.astype(jnp.float32) + jnp.dot(poly, matrix, preferred_element_type=jnp.float32)).astype(jnp.bfloat16)
    return matrix

def reference(grads, momentum, weights, owners, vec_grads, vec_params, vec_m, vec_v):

    def add_partial(position, total):
        return total + grads[position].astype(jnp.float32)
    gradient = lax.fori_loop(0, N_FSDP, add_partial, jnp.zeros((LAYERS, HD, D), jnp.float32))
    positions = jnp.arange(LAYERS)
    earlier = (owners[None, :] == owners[:, None]) & (positions[None, :] < positions[:, None])
    index = (owners * OWN_MAX + lax.optimization_barrier(jnp.sum(earlier.astype(jnp.int32), axis=1))).astype(jnp.int32)
    moment = BETA * momentum[index] + gradient
    new_momentum = momentum.at[index].set(moment)
    blend = gradient + BETA * moment
    norms = jnp.sqrt(lax.optimization_barrier(jnp.sum(blend * blend, axis=(1, 2))))
    start = (blend / (norms + EPS_NORM)[:, None, None]).astype(jnp.bfloat16)
    ortho = lax.map(newton_schulz, start)
    update = (0.2 * math.sqrt(D) * ortho.astype(jnp.float32)).astype(jnp.bfloat16)
    new_weights = weights * (1.0 - MUON_RATE * DECAY) - MUON_RATE * update.astype(jnp.float32)
    vec_sum = lax.optimization_barrier(jnp.sum(vec_grads, axis=0))
    new_vec_m = ADAM_ONE * vec_m + (1.0 - ADAM_ONE) * vec_sum
    new_vec_v = ADAM_TWO * vec_v + (1.0 - ADAM_TWO) * vec_sum * vec_sum
    ratio = new_vec_m / BIAS_ONE / (jnp.sqrt(new_vec_v / BIAS_TWO) + ADAM_EPS)
    new_vec_params = vec_params - VEC_RATE * (ratio + DECAY * vec_params)
    return (new_weights, update, new_momentum, new_vec_params, new_vec_m, new_vec_v)
```

```python
import math

import jax
import jax.numpy as jnp
from jax import lax
from jax.experimental import pallas as pl
from jax.experimental.pallas import tpu as pltpu
from jax.sharding import PartitionSpec as P

OWN_MAX = 2
NS_ITERS = 3

BETA = 0.5
EPS_NORM = 1e-07
COEF_A = 3.4445
COEF_B = -4.775
COEF_C = 2.0315
MUON_RATE = 0.02
DECAY = 0.1
VEC_RATE = 0.01
ADAM_ONE = 0.9
ADAM_TWO = 0.95
BIAS_ONE = 1.0 - 0.9**10
BIAS_TWO = 1.0 - 0.95**10
ADAM_EPS = 1e-08

RING = 4
PIECES = 2
ROWS = 192
WIDTH = 1280
FULL = RING * ROWS
HALF = ROWS // 2
QUARTER = ROWS // 4
COLS = WIDTH // PIECES
OUT_COLS = WIDTH // 32
SEG = 5
MESH = pl.DeviceIdType.MESH
BF = jnp.bfloat16
F32 = jnp.float32

T_MINUS, T_PLUS, D_MINUS, D_PLUS, S_MINUS, S_PLUS = range(6)
SEND_UNIT = ((2, 0), (2, 1), (3, 1), (1, 0), (3, 0), (1, 1))


def kernel(
    g_hbm, m_hbm, owners, v_hbm, upd_out, sel_out, vsum_out,
    own, par, r1, r2, rr, o2, sm, sg, mf, mb0, mb1, mb2, mb3, grid, gx, gs, xm0, xm1, xa, xb, gram, am, bm, ub, us, ur, vin, vbuf, va, vs, vb,
    sidx, wgt,
    own_sem, par_send, par_recv, mf_sem, mb_send, mb_recv,
    s1_send, s1_recv, s2_send, s2_recv, y_send, y_recv, yf_send, yf_recv,
    ag_send, ag_recv, gx_send, gx_recv, ut_send, ut_recv,
    keep_sem, stay_sem, v_sem, va_send, va_recv, vb_send, vb_recv,
):
    f = lax.axis_index("fsdp")
    t = lax.axis_index("tp")
    x, z, c = f // 8, (f // 2) % RING, f % 2
    chip = f // 2
    waits = []
    xm = (xm0, xm1)
    mb = (mb0, mb1, mb2, mb3)

    def fid(xx, zz, cc):
        return (xx * RING + zz) * 2 + cc

    def near(axis, step):
        if axis == 0:
            return (fid((x + step) % RING, z, c), t)
        return (fid(x, (z + step) % RING, c), t)

    partner = (fid(x, z, 1 - c), t)

    def remote(src, dst, send, recv, to):
        copy = pltpu.make_async_remote_copy(
            src_ref=src, dst_ref=dst, send_sem=send, recv_sem=recv, device_id=to, device_id_type=MESH
        )
        copy.start()
        waits.append(copy)
        return copy

    def unit_src(p, q, e, half, core):
        rows = pl.ds(q * HALF + half * QUARTER, QUARTER)
        cols = pl.ds(p * COLS, COLS)
        if q == 0:
            return g_hbm.at[(x + e) % RING, :, core, rows, cols]
        return g_hbm.at[:, (z + e) % RING, core, rows, cols]

    order = [SEND_UNIT[k] for k in range(6)] + [(0, 0), (0, 1)]
    own_copy = {}
    mload = pltpu.make_async_copy(m_hbm, mf, mf_sem)
    mload.start()
    for p in range(PIECES):
        for e, half in order:
            for q in range(2):
                cp = pltpu.make_async_copy(unit_src(p, q, e, half, c), own.at[p, q, e, half], own_sem.at[p, q, e, half])
                cp.start()
                own_copy[p, q, e, half] = cp
    vload = pltpu.make_async_copy(v_hbm, vin.at[pl.ds(0, 640)], v_sem)
    vload.start()

    barrier = pltpu.get_barrier_semaphore()

    def greet(d, carry):
        pl.semaphore_signal(barrier, inc=1, device_id=((f + d) % 32, t), device_id_type=MESH)
        return carry

    lax.fori_loop(1, 32, greet, 0)
    for d in range(1, RING):
        pl.semaphore_signal(barrier, inc=1, device_id=(f, (t + d) % RING), device_id_type=MESH)

    def look(k, carry):
        n0, n1, k0, k1, k2, k3 = carry
        rel = owners[k] - 2 * chip
        is0, is1 = rel == 0, rel == 1
        slot = jnp.where(is1, 2 + jnp.minimum(n1, 1), jnp.minimum(n0, 1))
        used = jnp.logical_or(is0, is1)
        sidx[k] = jnp.where(used, slot, 0)
        wgt[k] = jnp.where(used, F32(1.0 / 6.0), F32(0.0))
        hit = jnp.where(used, slot, -1)
        return (
            n0 + jnp.where(is0, 1, 0),
            n1 + jnp.where(is1, 1, 0),
            jnp.where(hit == 0, k, k0),
            jnp.where(hit == 1, k, k1),
            jnp.where(hit == 2, k, k2),
            jnp.where(hit == 3, k, k3),
        )

    zero = jnp.int32(0)
    _, _, k0, k1, k2, k3 = lax.fori_loop(0, 32, look, (zero,) * 6)

    mload.wait()

    for i in range(4):
        for s in range(2):
            mb[i][2 * c + s] = mf[s, pl.ds(i * QUARTER, QUARTER), :].astype(BF)
    pl.semaphore_wait(barrier, 31 + RING - 1)

    mb_copy = {}
    par_copy = {}

    def give(p, e, half, q):
        par_copy[p, q, e, half] = remote(
            unit_src(p, q, e, half, 1 - c), par.at[p, q, e, half],
            par_send.at[p, q, e, half], par_recv.at[p, q, e, half], partner,
        )

    for p in range(PIECES):
        for e, half in order:
            for q in range(2):
                if (q, half) not in mb_copy:
                    part = mb[2 * q + half].at[pl.ds(2 * c, 2)]
                    mb_copy[q, half] = remote(part, part, mb_send.at[q, half], mb_recv.at[q, half], partner)
                give(p, e, half, q)

    mb_done = set()

    def unit_sum(p, q, e, half, extra=None):
        own_copy[p, q, e, half].wait()
        if (q, half) not in mb_done:
            mb_done.add((q, half))
            mb_copy[q, half].wait_recv()
        par_copy[p, q, e, half].wait_recv()
        cols = pl.ds(p * COLS, COLS)

        def body(j, carry):
            if q == 0:
                k = ((x + e) % RING) * 8 + 2 * j + c
            else:
                k = j * 8 + 2 * ((z + e) % RING) + c
            acc = own[p, q, e, half, j].astype(F32) + par[p, q, e, half, j].astype(F32)
            acc += wgt[k] * mb[2 * q + half][sidx[k], :, cols].astype(F32)
            if extra is not None:
                acc += r1[p, q, extra, j].astype(F32)
            own[p, q, e, half, j] = acc.astype(BF)
            return carry

        if extra is not None:
            for j in range(RING):
                body(j, 0)
        else:
            lax.fori_loop(0, RING, body, 0)

    copy1 = {}
    copy2 = {}

    def first_send(p, q, kind):
        e, half = SEND_UNIT[kind]
        copy1[p, q, kind] = remote(
            own.at[p, q, e, half], r1.at[p, q, kind], s1_send.at[p, q, kind], s1_recv.at[p, q, kind],
            near(q, -1 if kind % 2 == 0 else 1),
        )

    def transit(p):
        for q in range(2):
            for kind in (T_MINUS, T_PLUS):
                unit_sum(p, q, *SEND_UNIT[kind])
                first_send(p, q, kind)

    def direct(p):
        for q in range(2):
            for kind in (D_MINUS, D_PLUS):
                unit_sum(p, q, *SEND_UNIT[kind])
                first_send(p, q, kind)

    def second(p):
        for q in range(2):
            for kind in (S_MINUS, S_PLUS):
                copy1[p, q, kind - 4].wait_recv()
                unit_sum(p, q, *SEND_UNIT[kind], extra=kind - 4)
                first_send(p, q, kind)

    ARRIVE = ((S_MINUS, D_PLUS), (S_PLUS, D_MINUS))

    def presum(p):
        for q in range(2):
            for half in range(2):
                kind = ARRIVE[half][1]
                copy1[p, q, kind].wait_recv()
                unit_sum(p, q, 0, half, extra=kind)

    def other_send(p, q, kind, src):
        copy2[p, q, kind] = remote(
            src, r2.at[p, q, kind], s2_send.at[p, q, kind], s2_recv.at[p, q, kind],
            near(1 - q, -1 if kind % 2 == 0 else 1),
        )

    def line_at(q, e):
        return ((z if q == 0 else x) + e) % RING

    def line_send(p, q, kind):
        e, half = SEND_UNIT[kind]
        other_send(p, q, kind, rr.at[p, q, half, line_at(q, e)])

    def line(p):
        for q in range(2):
            for half in range(2):
                copy1[p, q, ARRIVE[half][0]].wait_recv()
                for j in range(RING):
                    acc = own[p, q, 0, half, j].astype(F32) + r1[p, q, ARRIVE[half][0], j].astype(F32)
                    rr[p, q, half, j] = acc.astype(BF)
                line_send(p, q, T_MINUS if half == 0 else T_PLUS)
        for q in range(2):
            for kind in (D_MINUS, D_PLUS):
                line_send(p, q, kind)

    def line_second(p):
        for q in range(2):
            for kind in (S_MINUS, S_PLUS):
                e, half = SEND_UNIT[kind]
                copy2[p, q, kind - 4].wait_recv()
                acc = rr[p, q, half, line_at(q, e)].astype(F32) + r2[p, q, kind - 4].astype(F32)
                o2[p, q, kind - 4] = acc.astype(BF)
                other_send(p, q, kind, o2.at[p, q, kind - 4])

    my_rows = pl.multiple_of(t * ROWS, ROWS)

    def finish(p):
        cols = pl.ds(p * COLS, COLS)
        for q in range(2):
            for half in range(2):
                copy2[p, q, ARRIVE[half][0]].wait_recv()
                copy2[p, q, ARRIVE[half][1]].wait_recv()
                acc = rr[p, q, half, line_at(q, 0)].astype(F32)
                acc += r2[p, q, ARRIVE[half][0]].astype(F32) + r2[p, q, ARRIVE[half][1]].astype(F32)
                value = acc.astype(BF)
                at = q * HALF + half * QUARTER
                sm[p, pl.ds(at, QUARTER), :] = value
                sg[pl.ds(at, QUARTER), cols] = value

    y_copy = {}
    yf_copy = {}
    y_near = ((f, (t + RING - 1) % RING), (f, (t + 1) % RING))

    def y_part(p, owner, half):
        at = pl.multiple_of(owner * ROWS + half * HALF, HALF)
        return xm[p].at[pl.ds(at, HALF), :]

    def y_start(p):
        for first in (True, False):
            for way in range(2):
                half = way if first else 1 - way
                part = sm.at[p, pl.ds(half * HALF, HALF), :]
                y_copy[p, way, half] = remote(part, y_part(p, t, half), y_send.at[p, way, half], y_recv.at[p, way, half], y_near[way])

    def y_forward(p):
        for way in range(2):
            y_copy[p, way, way].wait_recv()
            part = y_part(p, (t + (1 if way == 0 else RING - 1)) % RING, way)
            yf_copy[p, way] = remote(part, part, yf_send.at[p, way], yf_recv.at[p, way], y_near[way])

    def y_wait(p):
        for way in range(2):
            y_copy[p, way, 1 - way].wait_recv()
            yf_copy[p, way].wait_recv()
        xm[p][pl.ds(my_rows, ROWS), :] = sm[p]

    ag = {}

    def ag_step(stage):
        if stage == 0:
            keep = pltpu.make_async_copy(sg, grid.at[x, z], keep_sem)
            keep.start()
            ag["keep"] = keep
        if stage == 2:
            ag["keep"].wait()
        for q in range(2):
            a1 = 1 - q
            for way in range(2):
                step = -1 if way == 0 else 1
                back = -step
                if stage % 2 == 0:
                    rows = pl.ds(q * HALF, HALF)
                    off = 0
                else:
                    ag[stage - 1, q, way].wait_recv()
                    rows = pl.ds(q * HALF + way * QUARTER, QUARTER)
                    off = back
                if stage < 2:
                    xx = x if a1 == 1 else (x + off) % RING
                    zz = z if a1 == 0 else (z + off) % RING
                    part = grid.at[xx, zz, rows]
                    axis = a1
                elif q == 0:
                    part = grid.at[(x + off) % RING, :, rows]
                    axis = 0
                else:
                    part = grid.at[:, (z + off) % RING, rows]
                    axis = 1
                src = sg.at[rows] if stage == 0 else part
                ag[stage, q, way] = remote(src, part, ag_send.at[stage, q, way], ag_recv.at[stage, q, way], near(axis, step))

    def ag_wait(stage):
        for q in range(2):
            for way in range(2):
                ag[stage, q, way].wait_recv()

    def v_split():
        vload.wait()
        vin[pl.ds(640, 8), :] = jnp.zeros((8, 128), F32)

        def body(s, carry):
            vbuf[s % RING, s // RING] = vin[pl.ds(SEG * s, 8), :]
            return carry

        lax.fori_loop(0, 128, body, 0)

    v_copy = {}

    def v_first():
        for d in range(1, RING):
            to = (t + d) % RING
            v_copy[d] = remote(vbuf.at[to], va.at[d - 1], va_send.at[d - 1], va_recv.at[d - 1], (f, to))

    def v_second():
        for d in range(1, RING):
            v_copy[d].wait_recv()

        def body(i, carry):
            rows = pl.ds(i * 8, 8)
            vs[rows] = vbuf[t, rows] + va[0, rows] + va[1, rows] + va[2, rows]
            return carry

        lax.fori_loop(0, 4, body, 0)

        def send(d, carry):
            to = (f + d) % 32
            pltpu.make_async_remote_copy(
                src_ref=vs.at[to], dst_ref=vb.at[d - 1], send_sem=vb_send.at[d - 1], recv_sem=vb_recv.at[d - 1],
                device_id=(to, t), device_id_type=MESH,
            ).start()
            return carry

        lax.fori_loop(1, 32, send, 0)

    def v_last():
        def arrive(d, carry):
            pltpu.make_async_remote_copy(
                src_ref=vs.at[f], dst_ref=vb.at[d - 1], send_sem=vb_send.at[d - 1], recv_sem=vb_recv.at[d - 1],
                device_id=((f + d) % 32, t), device_id_type=MESH,
            ).wait()
            return carry

        lax.fori_loop(1, 32, arrive, 0)
        vsum_out[...] = lax.fori_loop(0, 31, lambda d, acc: acc + vb[d], vs[f])

    NT = (((1,), (1,)), ((), ()))
    BLOCK = 256

    def gram_piece(src, add):
        def body(r, carry):
            rows = pl.ds(pl.multiple_of(r * BLOCK, BLOCK), BLOCK)
            d = lax.dot_general(src[rows, :], src[...], NT, preferred_element_type=F32)
            if add:
                d += gram[rows, :]
            gram[rows, :] = d
            return carry

        lax.fori_loop(0, FULL // BLOCK, body, 0)

    def to_a(scale):
        def body(r, carry):
            rows = pl.ds(pl.multiple_of(r * HALF, HALF), HALF)
            am[rows, :] = (gram[rows, :] * scale).astype(BF) if scale is not None else gram[rows, :].astype(BF)
            return carry

        lax.fori_loop(0, FULL // HALF, body, 0)

    def poly():
        def body(r, carry):
            rows = pl.ds(pl.multiple_of(r * BLOCK, BLOCK), BLOCK)
            block = am[rows, :]
            square = jnp.dot(block, am[...], preferred_element_type=F32)
            bm[rows, :] = (COEF_B * block.astype(F32) + COEF_C * square).astype(BF)
            return carry

        lax.fori_loop(0, FULL // BLOCK, body, 0)

    def advance(src, dst, scale, p=None):
        cols = slice(None) if p is None else pl.ds(p * COLS, COLS)
        def body(r, carry):
            rows = pl.ds(pl.multiple_of(r * BLOCK, BLOCK), BLOCK)
            d = jnp.dot(bm[rows, :], src[...], preferred_element_type=F32)
            d = COEF_A * src[rows, :].astype(F32) + d
            dst[rows, cols] = (d * scale).astype(BF) if scale is not None else d.astype(BF)
            return carry

        lax.fori_loop(0, FULL // BLOCK, body, 0)

    transit(0)
    v_split()
    direct(0)
    v_first()
    transit(1)
    second(0)
    direct(1)
    presum(0)
    v_second()
    line(0)
    second(1)
    line_second(0)
    presum(1)
    finish(0)
    y_start(0)
    line(1)
    y_forward(0)
    line_second(1)
    y_wait(0)
    finish(1)
    y_start(1)
    ag_step(0)
    gram_piece(xm[0], False)
    y_forward(1)
    ag_step(1)
    v_last()
    ag_wait(1)
    ag_step(2)
    y_wait(1)
    gram_piece(xm[1], True)

    def trace(r, acc):
        rows = pl.ds(pl.multiple_of(r * HALF, HALF), HALF)
        ri = lax.broadcasted_iota(jnp.int32, (HALF, FULL), 0) + r * HALF
        ci = lax.broadcasted_iota(jnp.int32, (HALF, FULL), 1)
        return acc + jnp.sum(jnp.where(ri == ci, gram[rows, :], 0.0), axis=0, keepdims=True)

    ss = jnp.sum(lax.fori_loop(0, FULL // HALF, trace, jnp.zeros((1, FULL), F32)), axis=1, keepdims=True)
    scale = 1.5 / (1.5 * jnp.sqrt(ss) + EPS_NORM)
    to_a(scale * scale)
    poly()
    for p in range(PIECES):
        advance(xm[p], xa, scale, p)
    gram_piece(xa, False)
    to_a(None)
    poly()
    advance(xa, xb, None)
    ag_step(3)
    gram_piece(xb, False)
    to_a(None)
    mine = pl.ds(my_rows, ROWS)
    block = am[mine, :]
    square = jnp.dot(block, am[...], preferred_element_type=F32)
    last = (COEF_B * block.astype(F32) + COEF_C * square).astype(BF)
    out = jnp.dot(last, xb[...], preferred_element_type=F32)
    ortho = (COEF_A * xb[mine, :].astype(F32) + out).astype(BF)
    upd = 0.2 * math.sqrt(WIDTH) * ortho.astype(F32)
    for b in range(WIDTH // 128):
        ub[pl.ds(b * 128, 128), :] = upd[:, b * 128 : (b + 1) * 128].T

    def pack(d, carry):
        us[d] = ub[pl.ds(pl.multiple_of(d * OUT_COLS, 8), OUT_COLS), :].astype(BF)
        return carry

    lax.fori_loop(0, 32, pack, 0)

    def give_columns(d):
        to = (f + d) % 32
        return pltpu.make_async_remote_copy(
            src_ref=us.at[to], dst_ref=ur.at[f], send_sem=ut_send.at[d - 1], recv_sem=ut_recv.at[d - 1],
            device_id=(to, t), device_id_type=MESH,
        )

    def send(d, carry):
        give_columns(d).start()
        return carry

    lax.fori_loop(1, 32, send, 0)
    stay = pltpu.make_async_copy(us.at[f], ur.at[f], stay_sem)
    stay.start()
    stay.wait()

    ag_wait(3)
    theirs = (jnp.where(c == 0, k2, k0), jnp.where(c == 0, k3, k1))
    ours = (jnp.where(c == 0, k0, k2), jnp.where(c == 0, k1, k3))
    for s in range(2):
        k = theirs[s]
        gs[s] = grid[k // 8, (k // 2) % RING]
        gx_copy = remote(gs.at[s], gx.at[s], gx_send.at[s], gx_recv.at[s], partner)
    for s in range(2):
        waits[-2 + s].wait_recv()
    for s in range(2):
        k = ours[s]
        here = grid[k // 8, (k // 2) % RING]
        sel_out[s] = jnp.where(k % 2 == c, here, gx[s])

    def take(d, carry):
        give_columns(d).wait()
        return carry

    lax.fori_loop(1, 32, take, 0)
    upd_out[...] = ur[...]
    for copy in waits:
        copy.wait_send()


def dma(*shape):
    return pltpu.SemaphoreType.DMA(shape)


def move(grads, momentum, owners, vec):
    units = (PIECES, 2, RING, 2)
    sends = (PIECES, 2, 6)
    scratch = [
        pltpu.VMEM((*units, RING, QUARTER, COLS), BF),
        pltpu.VMEM((*units, RING, QUARTER, COLS), BF),
        pltpu.VMEM((*sends, RING, QUARTER, COLS), BF),
        pltpu.VMEM((*sends, QUARTER, COLS), BF),
        pltpu.VMEM((PIECES, 2, 2, RING, QUARTER, COLS), BF),
        pltpu.VMEM((PIECES, 2, 2, QUARTER, COLS), BF),
        pltpu.VMEM((PIECES, ROWS, COLS), BF),
        pltpu.VMEM((ROWS, WIDTH), BF),
        pltpu.VMEM((2, ROWS, WIDTH), F32),
        *[pltpu.VMEM((4, QUARTER, WIDTH), BF)] * 4,
        pltpu.VMEM((RING, RING, ROWS, WIDTH), BF),
        pltpu.VMEM((2, ROWS, WIDTH), BF),
        pltpu.VMEM((2, ROWS, WIDTH), BF),
        *[pltpu.VMEM((FULL, COLS), BF)] * PIECES,
        pltpu.VMEM((FULL, WIDTH), BF),
        pltpu.VMEM((FULL, WIDTH), BF),
        pltpu.VMEM((FULL, FULL), F32),
        pltpu.VMEM((FULL, FULL), BF),
        pltpu.VMEM((FULL, FULL), BF),
        pltpu.VMEM((WIDTH, ROWS), F32),
        pltpu.VMEM((32, OUT_COLS, ROWS), BF),
        pltpu.VMEM((32, OUT_COLS, ROWS), BF),
        pltpu.VMEM((648, 128), F32),
        pltpu.VMEM((RING, 32, 8, 128), F32),
        pltpu.VMEM((3, 32, 8, 128), F32),
        pltpu.VMEM((32, 8, 128), F32),
        pltpu.VMEM((31, 8, 128), F32),
        pltpu.SMEM((32,), jnp.int32),
        pltpu.SMEM((32,), F32),
        dma(*units), dma(*units), dma(*units),
        pltpu.SemaphoreType.DMA, dma(2, 2), dma(2, 2),
        dma(*sends), dma(*sends), dma(*sends), dma(*sends),
        dma(PIECES, 2, 2), dma(PIECES, 2, 2), dma(PIECES, 2), dma(PIECES, 2),
        dma(4, 2, 2), dma(4, 2, 2), dma(2), dma(2), dma(31), dma(31),
        pltpu.SemaphoreType.DMA, pltpu.SemaphoreType.DMA, pltpu.SemaphoreType.DMA, dma(3), dma(3), dma(31), dma(31),
    ]
    any_space = pl.BlockSpec(memory_space=pl.ANY)
    vmem = pl.BlockSpec(memory_space=pltpu.VMEM)
    return pl.pallas_call(
        kernel,
        out_shape=(
            jax.ShapeDtypeStruct((32, OUT_COLS, ROWS), BF),
            jax.ShapeDtypeStruct((2, ROWS, WIDTH), BF),
            jax.ShapeDtypeStruct((8, 128), F32),
        ),
        in_specs=[any_space, any_space, pl.BlockSpec(memory_space=pltpu.SMEM), any_space],
        out_specs=(vmem, vmem, vmem),
        scratch_shapes=scratch,
        compiler_params=pltpu.CompilerParams(
            collective_id=0, has_side_effects=True, vmem_limit_bytes=63_000_000
        ),
    )(grads, momentum, owners, vec)


def local(grads, momentum, weights, owners, vec_grads, vec_params, vec_m, vec_v):
    update_t, sums, vec_tile = move(
        grads.reshape(RING, RING, 2, ROWS, WIDTH), momentum, owners, vec_grads.reshape(640, 128)
    )
    slot_owner = lax.axis_index("fsdp")
    count = jnp.sum((owners == slot_owner).astype(jnp.int32))
    used = jnp.arange(OWN_MAX) < count
    moment = momentum * F32(1.0 / 3.0) + sums.astype(F32)
    new_momentum = jnp.where(used[:, None, None], moment, momentum)
    update = jnp.swapaxes(update_t, 1, 2)
    new_weights = weights * (1.0 - MUON_RATE * DECAY) - MUON_RATE * update.astype(F32)
    vec_sum = vec_tile[:SEG].reshape(SEG * 128)
    new_vec_m = ADAM_ONE * vec_m + (1.0 - ADAM_ONE) * vec_sum
    new_vec_v = ADAM_TWO * vec_v + (1.0 - ADAM_TWO) * vec_sum * vec_sum
    ratio = new_vec_m / BIAS_ONE / (jnp.sqrt(new_vec_v / BIAS_TWO) + ADAM_EPS)
    new_vec_params = vec_params - VEC_RATE * (ratio + DECAY * vec_params)
    return (new_weights, update, new_momentum, new_vec_params, new_vec_m, new_vec_v)


def solution(mesh):
    placed = (
        P("fsdp", None, "tp", None),
        P("fsdp", "tp", None),
        P(None, "tp", "fsdp"),
        P(),
        P(("fsdp", "tp"), None),
        P(("fsdp", "tp")),
        P(("fsdp", "tp")),
        P(("fsdp", "tp")),
    )
    return jax.shard_map(
        local,
        mesh=mesh,
        in_specs=placed,
        out_specs=(
            P(None, "tp", "fsdp"),
            P(None, "tp", "fsdp"),
            P("fsdp", "tp", None),
            P(("fsdp", "tp")),
            P(("fsdp", "tp")),
            P(("fsdp", "tp")),
        ),
        check_vma=False,
    )
```

```python
import math

import jax
import jax.numpy as jnp
from jax import lax
from jax.experimental import pallas as pl
from jax.experimental.pallas import tpu as pltpu
from jax.sharding import PartitionSpec as P

OWN_MAX = 2
NS_ITERS = 3

BETA = 0.5
EPS_NORM = 1e-07
COEF_A = 3.4445
COEF_B = -4.775
COEF_C = 2.0315
MUON_RATE = 0.02
DECAY = 0.1
VEC_RATE = 0.01
ADAM_ONE = 0.9
ADAM_TWO = 0.95
BIAS_ONE = 1.0 - 0.9**10
BIAS_TWO = 1.0 - 0.95**10
ADAM_EPS = 1e-08

RING = 4
PIECES = 2
ROWS = 192
WIDTH = 1280
FULL = RING * ROWS
HALF = ROWS // 2
QUARTER = ROWS // 4
COLS = WIDTH // PIECES
OUT_COLS = WIDTH // 32
SEG = 5
MESH = pl.DeviceIdType.MESH
BF = jnp.bfloat16
F32 = jnp.float32

T_MINUS, T_PLUS, D_MINUS, D_PLUS, S_MINUS, S_PLUS = range(6)
SEND_UNIT = ((2, 0), (2, 1), (3, 1), (1, 0), (3, 0), (1, 1))


def kernel(
    g_hbm, m_hbm, owners, v_hbm, upd_out, nm_out, vsum_out,
    own, par, r1, r2, rr, o2, sm, mf, mb0, mb1, mb2, mb3, l00, l01, l10, l11, ct, r3, xm0, xm1, xa, xb, gram, am, bm, ub, us, ur, vin, vbuf, va, vs, vb,
    sidx, wgt,
    own_sem, par_send, par_recv, mf_sem, mb_send, mb_recv,
    s1_send, s1_recv, s2_send, s2_recv, y_send, y_recv, yf_send, yf_recv,
    ag_send, ag_recv, gx_send, gx_recv, s3_send, s3_recv, ut_send, ut_recv,
    keep_sem, stay_sem, v_sem, va_send, va_recv, vb_send, vb_recv,
):
    f = lax.axis_index("fsdp")
    t = lax.axis_index("tp")
    x, z, c = f // 8, (f // 2) % RING, f % 2
    chip = f // 2
    waits = []
    xm = (xm0, xm1)
    gather = ((l00, l01), (l10, l11))
    mb = (mb0, mb1, mb2, mb3)

    def fid(xx, zz, cc):
        return (xx * RING + zz) * 2 + cc

    def near(axis, step):
        if axis == 0:
            return (fid((x + step) % RING, z, c), t)
        return (fid(x, (z + step) % RING, c), t)

    partner = (fid(x, z, 1 - c), t)

    def remote(src, dst, send, recv, to):
        copy = pltpu.make_async_remote_copy(
            src_ref=src, dst_ref=dst, send_sem=send, recv_sem=recv, device_id=to, device_id_type=MESH
        )
        copy.start()
        waits.append(copy)
        return copy

    barrier = pltpu.get_barrier_semaphore()

    def greet(d, carry):
        pl.semaphore_signal(barrier, inc=1, device_id=((f + d) % 32, t), device_id_type=MESH)
        return carry

    lax.fori_loop(1, 32, greet, 0)
    for d in range(1, RING):
        pl.semaphore_signal(barrier, inc=1, device_id=(f, (t + d) % RING), device_id_type=MESH)

    def unit_src(p, q, e, half, core):
        rows = pl.ds(q * HALF + half * QUARTER, QUARTER)
        cols = pl.ds(p * COLS, COLS)
        if q == 0:
            return g_hbm.at[(x + e) % RING, :, core, rows, cols]
        return g_hbm.at[:, (z + e) % RING, core, rows, cols]

    order = [SEND_UNIT[k] for k in range(6)] + [(0, 0), (0, 1)]
    own_copy = {}
    mload = pltpu.make_async_copy(m_hbm, mf, mf_sem)
    mload.start()
    for p in range(PIECES):
        for e, half in order:
            for q in range(2):
                cp = pltpu.make_async_copy(unit_src(p, q, e, half, c), own.at[p, q, e, half], own_sem.at[p, q, e, half])
                cp.start()
                own_copy[p, q, e, half] = cp
    vload = pltpu.make_async_copy(v_hbm, vin.at[pl.ds(0, 640)], v_sem)
    vload.start()

    def look(k, carry):
        n0, n1 = carry
        rel = owners[k] - 2 * chip
        is0, is1 = rel == 0, rel == 1
        slot = jnp.where(is1, 2 + jnp.minimum(n1, 1), jnp.minimum(n0, 1))
        used = jnp.logical_or(is0, is1)
        sidx[k] = jnp.where(used, slot, 0)
        wgt[k] = jnp.where(used, F32(1.0 / 6.0), F32(0.0))
        return n0 + jnp.where(is0, 1, 0), n1 + jnp.where(is1, 1, 0)

    zero = jnp.int32(0)
    lax.fori_loop(0, 32, look, (zero, zero))

    def find_owned():
        names = [(1, e) for e in range(RING)] + [(0, e) for e in range(1, RING)]
        ids = [fid((x + e) % RING, z, c) if axis == 0 else fid(x, (z + e) % RING, c) for axis, e in names]

        def body(k, carry):
            new = []
            for o, (n, ka, kb) in zip(ids, carry):
                hit = owners[k] == o
                ka = jnp.where(jnp.logical_and(hit, n == 0), k, ka)
                kb = jnp.where(jnp.logical_and(hit, n == 1), k, kb)
                new.append((n + jnp.where(hit, 1, 0), ka, kb))
            return tuple(new)

        got = lax.fori_loop(0, 32, body, ((zero, zero - 1, zero - 1),) * len(ids))
        held = {name: g[1:] for name, g in zip(names, got)}
        held[0, 0] = held[1, 0]
        return held

    mload.wait()

    for i in range(4):
        for s in range(2):
            mb[i][2 * c + s] = mf[s, pl.ds(i * QUARTER, QUARTER), :].astype(BF)
    pl.semaphore_wait(barrier, 31 + RING - 1)

    mb_copy = {}
    par_copy = {}

    def give(p, e, half, q):
        par_copy[p, q, e, half] = remote(
            unit_src(p, q, e, half, 1 - c), par.at[p, q, e, half],
            par_send.at[p, q, e, half], par_recv.at[p, q, e, half], partner,
        )

    for p in range(PIECES):
        for e, half in order:
            for q in range(2):
                if (q, half) not in mb_copy:
                    part = mb[2 * q + half].at[pl.ds(2 * c, 2)]
                    mb_copy[q, half] = remote(part, part, mb_send.at[q, half], mb_recv.at[q, half], partner)
                give(p, e, half, q)

    mb_done = set()

    def unit_sum(p, q, e, half, extra=None):
        own_copy[p, q, e, half].wait()
        if (q, half) not in mb_done:
            mb_done.add((q, half))
            mb_copy[q, half].wait_recv()
        par_copy[p, q, e, half].wait_recv()
        cols = pl.ds(p * COLS, COLS)

        def body(j, carry):
            if q == 0:
                k = ((x + e) % RING) * 8 + 2 * j + c
            else:
                k = j * 8 + 2 * ((z + e) % RING) + c
            acc = own[p, q, e, half, j].astype(F32) + par[p, q, e, half, j].astype(F32)
            acc += wgt[k] * mb[2 * q + half][sidx[k], :, cols].astype(F32)
            if extra is not None:
                acc += r1[p, q, extra, j].astype(F32)
            own[p, q, e, half, j] = acc.astype(BF)
            return carry

        if extra is not None:
            for j in range(RING):
                body(j, 0)
        else:
            lax.fori_loop(0, RING, body, 0)

    copy1 = {}
    copy2 = {}

    def first_send(p, q, kind):
        e, half = SEND_UNIT[kind]
        copy1[p, q, kind] = remote(
            own.at[p, q, e, half], r1.at[p, q, kind], s1_send.at[p, q, kind], s1_recv.at[p, q, kind],
            near(q, -1 if kind % 2 == 0 else 1),
        )

    def transit(p):
        for q in range(2):
            for kind in (T_MINUS, T_PLUS):
                unit_sum(p, q, *SEND_UNIT[kind])
                first_send(p, q, kind)

    def direct(p):
        for q in range(2):
            for kind in (D_MINUS, D_PLUS):
                unit_sum(p, q, *SEND_UNIT[kind])
                first_send(p, q, kind)

    def second(p):
        for q in range(2):
            for kind in (S_MINUS, S_PLUS):
                copy1[p, q, kind - 4].wait_recv()
                unit_sum(p, q, *SEND_UNIT[kind], extra=kind - 4)
                first_send(p, q, kind)

    ARRIVE = ((S_MINUS, D_PLUS), (S_PLUS, D_MINUS))

    def presum(p):
        for q in range(2):
            for half in range(2):
                kind = ARRIVE[half][1]
                copy1[p, q, kind].wait_recv()
                unit_sum(p, q, 0, half, extra=kind)

    def other_send(p, q, kind, src):
        copy2[p, q, kind] = remote(
            src, r2.at[p, q, kind], s2_send.at[p, q, kind], s2_recv.at[p, q, kind],
            near(1 - q, -1 if kind % 2 == 0 else 1),
        )

    def line_at(q, e):
        return ((z if q == 0 else x) + e) % RING

    def line_send(p, q, kind):
        e, half = SEND_UNIT[kind]
        other_send(p, q, kind, rr.at[p, q, half, line_at(q, e)])

    def line(p):
        for q in range(2):
            for half in range(2):
                copy1[p, q, ARRIVE[half][0]].wait_recv()
                for j in range(RING):
                    acc = own[p, q, 0, half, j].astype(F32) + r1[p, q, ARRIVE[half][0], j].astype(F32)
                    rr[p, q, half, j] = acc.astype(BF)
                line_send(p, q, T_MINUS if half == 0 else T_PLUS)
        for q in range(2):
            for kind in (D_MINUS, D_PLUS):
                line_send(p, q, kind)

    def line_second(p):
        for q in range(2):
            for kind in (S_MINUS, S_PLUS):
                e, half = SEND_UNIT[kind]
                copy2[p, q, kind - 4].wait_recv()
                acc = rr[p, q, half, line_at(q, e)].astype(F32) + r2[p, q, kind - 4].astype(F32)
                o2[p, q, kind - 4] = acc.astype(BF)
                other_send(p, q, kind, o2.at[p, q, kind - 4])

    my_rows = pl.multiple_of(t * ROWS, ROWS)

    def finish(p):
        for q in range(2):
            for half in range(2):
                copy2[p, q, ARRIVE[half][0]].wait_recv()
                copy2[p, q, ARRIVE[half][1]].wait_recv()
                acc = rr[p, q, half, line_at(q, 0)].astype(F32)
                acc += r2[p, q, ARRIVE[half][0]].astype(F32) + r2[p, q, ARRIVE[half][1]].astype(F32)
                value = acc.astype(BF)
                at = q * HALF + half * QUARTER
                sm[p, pl.ds(at, QUARTER), :] = value

    y_copy = {}
    yf_copy = {}
    y_near = ((f, (t + RING - 1) % RING), (f, (t + 1) % RING))

    def y_part(p, owner, half):
        at = pl.multiple_of(owner * ROWS + half * HALF, HALF)
        return xm[p].at[pl.ds(at, HALF), :]

    def y_start(p):
        for first in (True, False):
            for way in range(2):
                half = way if first else 1 - way
                part = sm.at[p, pl.ds(half * HALF, HALF), :]
                y_copy[p, way, half] = remote(part, y_part(p, t, half), y_send.at[p, way, half], y_recv.at[p, way, half], y_near[way])

    def y_forward(p):
        for way in range(2):
            y_copy[p, way, way].wait_recv()
            part = y_part(p, (t + (1 if way == 0 else RING - 1)) % RING, way)
            yf_copy[p, way] = remote(part, part, yf_send.at[p, way], yf_recv.at[p, way], y_near[way])

    def y_wait(p):
        for way in range(2):
            y_copy[p, way, 1 - way].wait_recv()
            yf_copy[p, way].wait_recv()
        xm[p][pl.ds(my_rows, ROWS), :] = sm[p]

    ag = {}

    def gather_step(stage, p):
        for q in range(2):
            at = x if q == 0 else z
            line_ref = gather[p][q]
            if stage == 0:
                keep = pltpu.make_async_copy(sm.at[p, pl.ds(q * HALF, HALF)], line_ref.at[c, at], keep_sem.at[p, q])
                keep.start()
                ag["keep", p, q] = keep
            for way in range(2):
                step = -1 if way == 0 else 1
                if stage == 0:
                    src, dst = sm.at[p, pl.ds(q * HALF, HALF)], line_ref.at[c, at]
                else:
                    ag[0, p, q, way].wait_recv()
                    src = dst = line_ref.at[c, (at - step) % RING, pl.ds(way * QUARTER, QUARTER)]
                ag[stage, p, q, way] = remote(
                    src, dst, ag_send.at[stage, p, q, way], ag_recv.at[stage, p, q, way], near(q, step)
                )

    def share(p):
        for q in range(2):
            ag["keep", p, q].wait()
            for way in range(2):
                ag[1, p, q, way].wait_recv()
            part = gather[p][q].at[c]
            ag["share", p, q] = remote(part, part, gx_send.at[p, q], gx_recv.at[p, q], partner)

    def pick(held, p, q, e, half, slot):
        k = held[1 - q, e][slot]
        there = jnp.maximum(k, 0)
        kx, kz = there // 8, (there // 2) % RING
        match = (kz == z) if q == 0 else (kx == x)
        weight = jnp.where(jnp.logical_and(k >= 0, match), F32(1.0), F32(0.0))
        block = gather[p][q][there % 2, kx if q == 0 else kz, pl.ds(half * QUARTER, QUARTER), :]
        return weight * block.astype(F32)

    copy3 = {}

    def pick_send(held, p, q, kind):
        e, half = SEND_UNIT[kind]
        for slot in range(2):
            acc = pick(held, p, q, e, half, slot)
            if kind >= 4:
                acc += r3[p, q, kind - 4, slot].astype(F32)
            ct[p, q, kind, slot] = acc.astype(BF)
        copy3[p, q, kind] = remote(
            ct.at[p, q, kind], r3.at[p, q, kind], s3_send.at[p, q, kind], s3_recv.at[p, q, kind],
            near(1 - q, -1 if kind % 2 == 0 else 1),
        )

    def pick_first(held, p):
        for q in range(2):
            ag["share", p, q].wait_recv()
            for kind in (T_MINUS, T_PLUS, D_MINUS, D_PLUS):
                pick_send(held, p, q, kind)

    def pick_second(held, p):
        for q in range(2):
            for kind in (S_MINUS, S_PLUS):
                copy3[p, q, kind - 4].wait_recv()
                pick_send(held, p, q, kind)

    def pick_last(held, p):
        cols = pl.ds(p * COLS, COLS)
        for q in range(2):
            for half in range(2):
                for kind in ARRIVE[half]:
                    copy3[p, q, kind].wait_recv()
                rows = pl.ds(q * HALF + half * QUARTER, QUARTER)
                for slot in range(2):
                    total = pick(held, p, q, 0, half, slot)
                    for kind in ARRIVE[half]:
                        total += r3[p, q, kind, slot].astype(F32)
                    old = mf[slot, rows, cols]
                    nm_out[slot, rows, cols] = jnp.where(held[1, 0][slot] >= 0, old * F32(1.0 / 3.0) + total, old)

    def v_split():
        vload.wait()
        vin[pl.ds(640, 8), :] = jnp.zeros((8, 128), F32)

        def body(s, carry):
            vbuf[s % RING, s // RING] = vin[pl.ds(SEG * s, 8), :]
            return carry

        lax.fori_loop(0, 128, body, 0)

    v_copy = {}

    def v_first():
        for d in range(1, RING):
            to = (t + d) % RING
            v_copy[d] = remote(vbuf.at[to], va.at[d - 1], va_send.at[d - 1], va_recv.at[d - 1], (f, to))

    def v_second():
        for d in range(1, RING):
            v_copy[d].wait_recv()

        def body(i, carry):
            rows = pl.ds(i * 8, 8)
            vs[rows] = vbuf[t, rows] + va[0, rows] + va[1, rows] + va[2, rows]
            return carry

        lax.fori_loop(0, 4, body, 0)

        def send(d, carry):
            to = (f + d) % 32
            pltpu.make_async_remote_copy(
                src_ref=vs.at[to], dst_ref=vb.at[d - 1], send_sem=vb_send.at[d - 1], recv_sem=vb_recv.at[d - 1],
                device_id=(to, t), device_id_type=MESH,
            ).start()
            return carry

        lax.fori_loop(1, 32, send, 0)

    def v_last():
        def arrive(d, carry):
            pltpu.make_async_remote_copy(
                src_ref=vs.at[f], dst_ref=vb.at[d - 1], send_sem=vb_send.at[d - 1], recv_sem=vb_recv.at[d - 1],
                device_id=((f + d) % 32, t), device_id_type=MESH,
            ).wait()
            return carry

        lax.fori_loop(1, 32, arrive, 0)
        vsum_out[...] = lax.fori_loop(0, 31, lambda d, acc: acc + vb[d], vs[f])

    NT = (((1,), (1,)), ((), ()))
    BLOCK = 256

    def gram_piece(src, add):
        def body(r, carry):
            rows = pl.ds(pl.multiple_of(r * BLOCK, BLOCK), BLOCK)
            d = lax.dot_general(src[rows, :], src[...], NT, preferred_element_type=F32)
            if add:
                d += gram[rows, :]
            gram[rows, :] = d
            return carry

        lax.fori_loop(0, FULL // BLOCK, body, 0)

    def to_a(scale):
        def body(r, carry):
            rows = pl.ds(pl.multiple_of(r * HALF, HALF), HALF)
            am[rows, :] = (gram[rows, :] * scale).astype(BF) if scale is not None else gram[rows, :].astype(BF)
            return carry

        lax.fori_loop(0, FULL // HALF, body, 0)

    def poly():
        def body(r, carry):
            rows = pl.ds(pl.multiple_of(r * BLOCK, BLOCK), BLOCK)
            block = am[rows, :]
            square = jnp.dot(block, am[...], preferred_element_type=F32)
            bm[rows, :] = (COEF_B * block.astype(F32) + COEF_C * square).astype(BF)
            return carry

        lax.fori_loop(0, FULL // BLOCK, body, 0)

    def advance(src, dst, scale, p=None):
        cols = slice(None) if p is None else pl.ds(p * COLS, COLS)
        def body(r, carry):
            rows = pl.ds(pl.multiple_of(r * BLOCK, BLOCK), BLOCK)
            d = jnp.dot(bm[rows, :], src[...], preferred_element_type=F32)
            d = COEF_A * src[rows, :].astype(F32) + d
            dst[rows, cols] = (d * scale).astype(BF) if scale is not None else d.astype(BF)
            return carry

        lax.fori_loop(0, FULL // BLOCK, body, 0)

    transit(0)
    v_split()
    direct(0)
    held = find_owned()
    v_first()
    transit(1)
    second(0)
    direct(1)
    presum(0)
    v_second()
    line(0)
    second(1)
    line_second(0)
    presum(1)
    line(1)
    finish(0)
    y_start(0)
    line_second(1)
    gather_step(0, 0)
    y_forward(0)
    finish(1)
    y_start(1)
    gather_step(1, 0)
    gather_step(0, 1)
    y_wait(0)
    gram_piece(xm[0], False)
    y_forward(1)
    gather_step(1, 1)
    share(0)
    v_last()
    y_wait(1)
    share(1)
    pick_first(held, 0)
    gram_piece(xm[1], True)
    pick_first(held, 1)

    def trace(r, acc):
        rows = pl.ds(pl.multiple_of(r * HALF, HALF), HALF)
        ri = lax.broadcasted_iota(jnp.int32, (HALF, FULL), 0) + r * HALF
        ci = lax.broadcasted_iota(jnp.int32, (HALF, FULL), 1)
        return acc + jnp.sum(jnp.where(ri == ci, gram[rows, :], 0.0), axis=0, keepdims=True)

    ss = jnp.sum(lax.fori_loop(0, FULL // HALF, trace, jnp.zeros((1, FULL), F32)), axis=1, keepdims=True)
    scale = 1.5 / (1.5 * jnp.sqrt(ss) + EPS_NORM)
    to_a(scale * scale)
    poly()
    for p in range(PIECES):
        advance(xm[p], xa, scale, p)
    pick_second(held, 0)
    gram_piece(xa, False)
    to_a(None)
    poly()
    pick_second(held, 1)
    advance(xa, xb, None)
    gram_piece(xb, False)
    to_a(None)
    mine = pl.ds(my_rows, ROWS)
    block = am[mine, :]
    square = jnp.dot(block, am[...], preferred_element_type=F32)
    last = (COEF_B * block.astype(F32) + COEF_C * square).astype(BF)
    out = jnp.dot(last, xb[...], preferred_element_type=F32)
    ortho = (COEF_A * xb[mine, :].astype(F32) + out).astype(BF)
    upd = 0.2 * math.sqrt(WIDTH) * ortho.astype(F32)
    for b in range(WIDTH // 128):
        ub[pl.ds(b * 128, 128), :] = upd[:, b * 128 : (b + 1) * 128].T

    def pack(d, carry):
        us[d] = ub[pl.ds(pl.multiple_of(d * OUT_COLS, 8), OUT_COLS), :].astype(BF)
        return carry

    lax.fori_loop(0, 32, pack, 0)

    def give_columns(d):
        to = (f + d) % 32
        return pltpu.make_async_remote_copy(
            src_ref=us.at[to], dst_ref=ur.at[f], send_sem=ut_send.at[d - 1], recv_sem=ut_recv.at[d - 1],
            device_id=(to, t), device_id_type=MESH,
        )

    def send(d, carry):
        give_columns(d).start()
        return carry

    lax.fori_loop(1, 32, send, 0)
    stay = pltpu.make_async_copy(us.at[f], ur.at[f], stay_sem)
    stay.start()
    stay.wait()

    for p in range(PIECES):
        pick_last(held, p)

    def take(d, carry):
        give_columns(d).wait()
        return carry

    lax.fori_loop(1, 32, take, 0)
    upd_out[...] = ur[...]
    for copy in waits:
        copy.wait_send()


def dma(*shape):
    return pltpu.SemaphoreType.DMA(shape)


def move(grads, momentum, owners, vec):
    units = (PIECES, 2, RING, 2)
    sends = (PIECES, 2, 6)
    scratch = [
        pltpu.VMEM((*units, RING, QUARTER, COLS), BF),
        pltpu.VMEM((*units, RING, QUARTER, COLS), BF),
        pltpu.VMEM((*sends, RING, QUARTER, COLS), BF),
        pltpu.VMEM((*sends, QUARTER, COLS), BF),
        pltpu.VMEM((PIECES, 2, 2, RING, QUARTER, COLS), BF),
        pltpu.VMEM((PIECES, 2, 2, QUARTER, COLS), BF),
        pltpu.VMEM((PIECES, ROWS, COLS), BF),
        pltpu.VMEM((2, ROWS, WIDTH), F32),
        *[pltpu.VMEM((4, QUARTER, WIDTH), BF)] * 4,
        *[pltpu.VMEM((2, RING, HALF, COLS), BF)] * (2 * PIECES),
        pltpu.VMEM((*sends, 2, QUARTER, COLS), BF),
        pltpu.VMEM((*sends, 2, QUARTER, COLS), BF),
        *[pltpu.VMEM((FULL, COLS), BF)] * PIECES,
        pltpu.VMEM((FULL, WIDTH), BF),
        pltpu.VMEM((FULL, WIDTH), BF),
        pltpu.VMEM((FULL, FULL), F32),
        pltpu.VMEM((FULL, FULL), BF),
        pltpu.VMEM((FULL, FULL), BF),
        pltpu.VMEM((WIDTH, ROWS), F32),
        pltpu.VMEM((32, OUT_COLS, ROWS), BF),
        pltpu.VMEM((32, OUT_COLS, ROWS), BF),
        pltpu.VMEM((648, 128), F32),
        pltpu.VMEM((RING, 32, 8, 128), F32),
        pltpu.VMEM((3, 32, 8, 128), F32),
        pltpu.VMEM((32, 8, 128), F32),
        pltpu.VMEM((31, 8, 128), F32),
        pltpu.SMEM((32,), jnp.int32),
        pltpu.SMEM((32,), F32),
        dma(*units), dma(*units), dma(*units),
        pltpu.SemaphoreType.DMA, dma(2, 2), dma(2, 2),
        dma(*sends), dma(*sends), dma(*sends), dma(*sends),
        dma(PIECES, 2, 2), dma(PIECES, 2, 2), dma(PIECES, 2), dma(PIECES, 2),
        dma(2, PIECES, 2, 2), dma(2, PIECES, 2, 2), dma(PIECES, 2), dma(PIECES, 2), dma(*sends), dma(*sends), dma(31), dma(31),
        dma(PIECES, 2), pltpu.SemaphoreType.DMA, pltpu.SemaphoreType.DMA, dma(3), dma(3), dma(31), dma(31),
    ]
    any_space = pl.BlockSpec(memory_space=pl.ANY)
    vmem = pl.BlockSpec(memory_space=pltpu.VMEM)
    return pl.pallas_call(
        kernel,
        out_shape=(
            jax.ShapeDtypeStruct((32, OUT_COLS, ROWS), BF),
            jax.ShapeDtypeStruct((2, ROWS, WIDTH), F32),
            jax.ShapeDtypeStruct((8, 128), F32),
        ),
        in_specs=[any_space, any_space, pl.BlockSpec(memory_space=pltpu.SMEM), any_space],
        out_specs=(vmem, vmem, vmem),
        scratch_shapes=scratch,
        compiler_params=pltpu.CompilerParams(
            collective_id=0, has_side_effects=True, vmem_limit_bytes=63_000_000
        ),
    )(grads, momentum, owners, vec)


def local(grads, momentum, weights, owners, vec_grads, vec_params, vec_m, vec_v):
    update_t, new_momentum, vec_tile = move(
        grads.reshape(RING, RING, 2, ROWS, WIDTH), momentum, owners, vec_grads.reshape(640, 128)
    )
    update = jnp.swapaxes(update_t, 1, 2)
    new_weights = weights * (1.0 - MUON_RATE * DECAY) - MUON_RATE * update.astype(F32)
    vec_sum = vec_tile[:SEG].reshape(SEG * 128)
    new_vec_m = ADAM_ONE * vec_m + (1.0 - ADAM_ONE) * vec_sum
    new_vec_v = ADAM_TWO * vec_v + (1.0 - ADAM_TWO) * vec_sum * vec_sum
    ratio = new_vec_m / BIAS_ONE / (jnp.sqrt(new_vec_v / BIAS_TWO) + ADAM_EPS)
    new_vec_params = vec_params - VEC_RATE * (ratio + DECAY * vec_params)
    return (new_weights, update, new_momentum, new_vec_params, new_vec_m, new_vec_v)


def solution(mesh):
    placed = (
        P("fsdp", None, "tp", None),
        P("fsdp", "tp", None),
        P(None, "tp", "fsdp"),
        P(),
        P(("fsdp", "tp"), None),
        P(("fsdp", "tp")),
        P(("fsdp", "tp")),
        P(("fsdp", "tp")),
    )
    return jax.shard_map(
        local,
        mesh=mesh,
        in_specs=placed,
        out_specs=(
            P(None, "tp", "fsdp"),
            P(None, "tp", "fsdp"),
            P("fsdp", "tp", None),
            P(("fsdp", "tp")),
            P(("fsdp", "tp")),
            P(("fsdp", "tp")),
        ),
        check_vma=False,
    )
```

```python
import math

import jax
import jax.numpy as jnp
from jax import lax
from jax.experimental import pallas as pl
from jax.experimental.pallas import tpu as pltpu
from jax.sharding import PartitionSpec as P

OWN_MAX = 2
NS_ITERS = 3

BETA = 0.5
EPS_NORM = 1e-07
COEF_A = 3.4445
COEF_B = -4.775
COEF_C = 2.0315
MUON_RATE = 0.02
DECAY = 0.1
VEC_RATE = 0.01
ADAM_ONE = 0.9
ADAM_TWO = 0.95
BIAS_ONE = 1.0 - 0.9**10
BIAS_TWO = 1.0 - 0.95**10
ADAM_EPS = 1e-08

RING = 4
WIDE = (512, 512, 256)
AT = (0, 512, 1024)
PIECES = len(WIDE)
ROWS = 192
WIDTH = 1280
FULL = RING * ROWS
HALF = ROWS // 2
QUARTER = ROWS // 4
OUT_COLS = WIDTH // 32
SEG = 5
MESH = pl.DeviceIdType.MESH
BF = jnp.bfloat16
F32 = jnp.float32

T_MINUS, T_PLUS, D_MINUS, D_PLUS, S_MINUS, S_PLUS = range(6)
SEND_UNIT = ((2, 0), (2, 1), (3, 1), (1, 0), (3, 0), (1, 1))


def kernel(
    g_hbm, m_hbm, owners, v_hbm, upd_out, nm_out, vsum_out,
    own, par, r1, r2, rr, o2, sm, mf, mb, gather, ct, r3, xm, xa, xb, gram, am, bm, ub, us, ur, vin, vbuf, va, vs, vb,
    sidx, wgt,
    own_sem, par_send, par_recv, mf_sem, mb_send, mb_recv,
    s1_send, s1_recv, s2_send, s2_recv, y_send, y_recv, yf_send, yf_recv,
    ag_send, ag_recv, gx_send, gx_recv, s3_send, s3_recv, ut_send, ut_recv,
    keep_sem, stay_sem, v_sem, va_send, va_recv, vb_send, vb_recv,
):
    f = lax.axis_index("fsdp")
    t = lax.axis_index("tp")
    x, z, c = f // 8, (f // 2) % RING, f % 2
    chip = f // 2
    waits = []

    def fid(xx, zz, cc):
        return (xx * RING + zz) * 2 + cc

    def near(axis, step):
        if axis == 0:
            return (fid((x + step) % RING, z, c), t)
        return (fid(x, (z + step) % RING, c), t)

    partner = (fid(x, z, 1 - c), t)

    def remote(src, dst, send, recv, to):
        copy = pltpu.make_async_remote_copy(
            src_ref=src, dst_ref=dst, send_sem=send, recv_sem=recv, device_id=to, device_id_type=MESH
        )
        copy.start()
        waits.append(copy)
        return copy

    barrier = pltpu.get_barrier_semaphore()

    def greet(d, carry):
        pl.semaphore_signal(barrier, inc=1, device_id=((f + d) % 32, t), device_id_type=MESH)
        return carry

    lax.fori_loop(1, 32, greet, 0)
    for d in range(1, RING):
        pl.semaphore_signal(barrier, inc=1, device_id=(f, (t + d) % RING), device_id_type=MESH)

    def unit_src(p, q, e, half, core):
        rows = pl.ds(q * HALF + half * QUARTER, QUARTER)
        cols = pl.ds(AT[p], WIDE[p])
        if q == 0:
            return g_hbm.at[(x + e) % RING, :, core, rows, cols]
        return g_hbm.at[:, (z + e) % RING, core, rows, cols]

    order = [SEND_UNIT[k] for k in range(6)] + [(0, 0), (0, 1)]
    own_copy = {}
    mload = pltpu.make_async_copy(m_hbm, mf, mf_sem)
    mload.start()
    def load(p):
        for e, half in order:
            for q in range(2):
                cp = pltpu.make_async_copy(unit_src(p, q, e, half, c), own[p].at[q, e, half], own_sem.at[p, q, e, half])
                cp.start()
                own_copy[p, q, e, half] = cp
    load(0)
    vload = pltpu.make_async_copy(v_hbm, vin.at[pl.ds(0, 640)], v_sem)
    vload.start()

    def look(k, carry):
        n0, n1 = carry
        rel = owners[k] - 2 * chip
        is0, is1 = rel == 0, rel == 1
        slot = jnp.where(is1, 2 + jnp.minimum(n1, 1), jnp.minimum(n0, 1))
        used = jnp.logical_or(is0, is1)
        sidx[k] = jnp.where(used, slot, 0)
        wgt[k] = jnp.where(used, F32(1.0 / 6.0), F32(0.0))
        return n0 + jnp.where(is0, 1, 0), n1 + jnp.where(is1, 1, 0)

    zero = jnp.int32(0)
    lax.fori_loop(0, 32, look, (zero, zero))

    def find_owned():
        names = [(1, e) for e in range(RING)] + [(0, e) for e in range(1, RING)]
        ids = [fid((x + e) % RING, z, c) if axis == 0 else fid(x, (z + e) % RING, c) for axis, e in names]

        def body(k, carry):
            new = []
            for o, (n, ka, kb) in zip(ids, carry):
                hit = owners[k] == o
                ka = jnp.where(jnp.logical_and(hit, n == 0), k, ka)
                kb = jnp.where(jnp.logical_and(hit, n == 1), k, kb)
                new.append((n + jnp.where(hit, 1, 0), ka, kb))
            return tuple(new)

        got = lax.fori_loop(0, 32, body, ((zero, zero - 1, zero - 1),) * len(ids))
        held = {name: g[1:] for name, g in zip(names, got)}
        held[0, 0] = held[1, 0]
        return held

    mload.wait()

    for p in range(PIECES):
        for i in range(4):
            for s in range(2):
                mb[p][i][2 * c + s] = mf[s, pl.ds(i * QUARTER, QUARTER), pl.ds(AT[p], WIDE[p])].astype(BF)
    pl.semaphore_wait(barrier, 31 + RING - 1)

    mb_copy = {}
    par_copy = {}

    def give(p, e, half, q):
        par_copy[p, q, e, half] = remote(
            unit_src(p, q, e, half, 1 - c), par[p].at[q, e, half],
            par_send.at[p, q, e, half], par_recv.at[p, q, e, half], partner,
        )

    def exchange(p):
        for e, half in order:
            for q in range(2):
                if (p, q, half) not in mb_copy:
                    part = mb[p][2 * q + half].at[pl.ds(2 * c, 2)]
                    mb_copy[p, q, half] = remote(part, part, mb_send.at[p, q, half], mb_recv.at[p, q, half], partner)
                give(p, e, half, q)

    mb_done = set()

    def unit_sum(p, q, e, half, extra=None):
        own_copy[p, q, e, half].wait()
        if (p, q, half) not in mb_done:
            mb_done.add((p, q, half))
            mb_copy[p, q, half].wait_recv()
        par_copy[p, q, e, half].wait_recv()
        def body(j, carry):
            if q == 0:
                k = ((x + e) % RING) * 8 + 2 * j + c
            else:
                k = j * 8 + 2 * ((z + e) % RING) + c
            acc = own[p][q, e, half, j].astype(F32) + par[p][q, e, half, j].astype(F32)
            acc += wgt[k] * mb[p][2 * q + half][sidx[k]].astype(F32)
            if extra is not None:
                acc += r1[p][q, extra, j].astype(F32)
            own[p][q, e, half, j] = acc.astype(BF)
            return carry

        if extra is not None:
            for j in range(RING):
                body(j, 0)
        else:
            lax.fori_loop(0, RING, body, 0)

    copy1 = {}
    copy2 = {}

    def first_send(p, q, kind):
        e, half = SEND_UNIT[kind]
        copy1[p, q, kind] = remote(
            own[p].at[q, e, half], r1[p].at[q, kind], s1_send.at[p, q, kind], s1_recv.at[p, q, kind],
            near(q, -1 if kind % 2 == 0 else 1),
        )

    def transit(p):
        for q in range(2):
            for kind in (T_MINUS, T_PLUS):
                unit_sum(p, q, *SEND_UNIT[kind])
                first_send(p, q, kind)

    def direct(p):
        for q in range(2):
            for kind in (D_MINUS, D_PLUS):
                unit_sum(p, q, *SEND_UNIT[kind])
                first_send(p, q, kind)

    def second(p):
        for q in range(2):
            for kind in (S_MINUS, S_PLUS):
                copy1[p, q, kind - 4].wait_recv()
                unit_sum(p, q, *SEND_UNIT[kind], extra=kind - 4)
                first_send(p, q, kind)

    ARRIVE = ((S_MINUS, D_PLUS), (S_PLUS, D_MINUS))

    def presum(p):
        for q in range(2):
            for half in range(2):
                kind = ARRIVE[half][1]
                copy1[p, q, kind].wait_recv()
                unit_sum(p, q, 0, half, extra=kind)

    def other_send(p, q, kind, src):
        copy2[p, q, kind] = remote(
            src, r2[p].at[q, kind], s2_send.at[p, q, kind], s2_recv.at[p, q, kind],
            near(1 - q, -1 if kind % 2 == 0 else 1),
        )

    def line_at(q, e):
        return ((z if q == 0 else x) + e) % RING

    def line_send(p, q, kind):
        e, half = SEND_UNIT[kind]
        other_send(p, q, kind, rr[p].at[q, half, line_at(q, e)])

    def line(p):
        for q in range(2):
            for half in range(2):
                copy1[p, q, ARRIVE[half][0]].wait_recv()
                for j in range(RING):
                    acc = own[p][q, 0, half, j].astype(F32) + r1[p][q, ARRIVE[half][0], j].astype(F32)
                    rr[p][q, half, j] = acc.astype(BF)
                line_send(p, q, T_MINUS if half == 0 else T_PLUS)
        for q in range(2):
            for kind in (D_MINUS, D_PLUS):
                line_send(p, q, kind)

    def line_second(p):
        for q in range(2):
            for kind in (S_MINUS, S_PLUS):
                e, half = SEND_UNIT[kind]
                copy2[p, q, kind - 4].wait_recv()
                acc = rr[p][q, half, line_at(q, e)].astype(F32) + r2[p][q, kind - 4].astype(F32)
                o2[p][q, kind - 4] = acc.astype(BF)
                other_send(p, q, kind, o2[p].at[q, kind - 4])

    my_rows = pl.multiple_of(t * ROWS, ROWS)

    def finish(p):
        for q in range(2):
            for half in range(2):
                copy2[p, q, ARRIVE[half][0]].wait_recv()
                copy2[p, q, ARRIVE[half][1]].wait_recv()
                acc = rr[p][q, half, line_at(q, 0)].astype(F32)
                acc += r2[p][q, ARRIVE[half][0]].astype(F32) + r2[p][q, ARRIVE[half][1]].astype(F32)
                value = acc.astype(BF)
                at = q * HALF + half * QUARTER
                sm[p][pl.ds(at, QUARTER), :] = value

    y_copy = {}
    yf_copy = {}
    y_near = ((f, (t + RING - 1) % RING), (f, (t + 1) % RING))

    def y_part(p, owner, half):
        at = pl.multiple_of(owner * ROWS + half * HALF, HALF)
        return xm[p].at[pl.ds(at, HALF), :]

    def y_start(p):
        for first in (True, False):
            for way in range(2):
                half = way if first else 1 - way
                part = sm[p].at[pl.ds(half * HALF, HALF), :]
                y_copy[p, way, half] = remote(part, y_part(p, t, half), y_send.at[p, way, half], y_recv.at[p, way, half], y_near[way])

    def y_forward(p):
        for way in range(2):
            y_copy[p, way, way].wait_recv()
            part = y_part(p, (t + (1 if way == 0 else RING - 1)) % RING, way)
            yf_copy[p, way] = remote(part, part, yf_send.at[p, way], yf_recv.at[p, way], y_near[way])

    def y_wait(p):
        for way in range(2):
            y_copy[p, way, 1 - way].wait_recv()
            yf_copy[p, way].wait_recv()
        xm[p][pl.ds(my_rows, ROWS), :] = sm[p][...]

    ag = {}

    def gather_step(stage, p):
        for q in range(2):
            at = x if q == 0 else z
            line_ref = gather[p][q]
            if stage == 0:
                keep = pltpu.make_async_copy(sm[p].at[pl.ds(q * HALF, HALF)], line_ref.at[c, at], keep_sem.at[p, q])
                keep.start()
                ag["keep", p, q] = keep
            for way in range(2):
                step = -1 if way == 0 else 1
                if stage == 0:
                    src, dst = sm[p].at[pl.ds(q * HALF, HALF)], line_ref.at[c, at]
                else:
                    ag[0, p, q, way].wait_recv()
                    src = dst = line_ref.at[c, (at - step) % RING, pl.ds(way * QUARTER, QUARTER)]
                ag[stage, p, q, way] = remote(
                    src, dst, ag_send.at[stage, p, q, way], ag_recv.at[stage, p, q, way], near(q, step)
                )

    def share(p):
        for q in range(2):
            ag["keep", p, q].wait()
            for way in range(2):
                ag[1, p, q, way].wait_recv()
            part = gather[p][q].at[c]
            ag["share", p, q] = remote(part, part, gx_send.at[p, q], gx_recv.at[p, q], partner)

    def pick(held, p, q, e, half, slot):
        k = held[1 - q, e][slot]
        there = jnp.maximum(k, 0)
        kx, kz = there // 8, (there // 2) % RING
        match = (kz == z) if q == 0 else (kx == x)
        block = gather[p][q][there % 2, kx if q == 0 else kz, pl.ds(half * QUARTER, QUARTER), :]
        return jnp.where(jnp.logical_and(k >= 0, match), block, jnp.zeros_like(block))

    copy3 = {}

    def pick_send(held, p, q, kind):
        e, half = SEND_UNIT[kind]
        for slot in range(2):
            acc = pick(held, p, q, e, half, slot)
            if kind >= 4:
                acc = (acc.astype(F32) + r3[p][q, kind - 4, slot].astype(F32)).astype(BF)
            ct[p][q, kind, slot] = acc
        copy3[p, q, kind] = remote(
            ct[p].at[q, kind], r3[p].at[q, kind], s3_send.at[p, q, kind], s3_recv.at[p, q, kind],
            near(1 - q, -1 if kind % 2 == 0 else 1),
        )

    def pick_first(held, p):
        for q in range(2):
            ag["share", p, q].wait_recv()
            for kind in (T_MINUS, T_PLUS, D_MINUS, D_PLUS):
                pick_send(held, p, q, kind)

    def pick_second(held, p):
        for q in range(2):
            for kind in (S_MINUS, S_PLUS):
                copy3[p, q, kind - 4].wait_recv()
                pick_send(held, p, q, kind)

    def pick_last(held, p):
        cols = pl.ds(AT[p], WIDE[p])
        for q in range(2):
            for half in range(2):
                for kind in ARRIVE[half]:
                    copy3[p, q, kind].wait_recv()
                rows = pl.ds(q * HALF + half * QUARTER, QUARTER)
                for slot in range(2):
                    total = pick(held, p, q, 0, half, slot).astype(F32)
                    for kind in ARRIVE[half]:
                        total += r3[p][q, kind, slot].astype(F32)
                    old = mf[slot, rows, cols]
                    nm_out[slot, rows, cols] = jnp.where(held[1, 0][slot] >= 0, old * F32(1.0 / 3.0) + total, old)

    def v_split():
        vload.wait()
        vin[pl.ds(640, 8), :] = jnp.zeros((8, 128), F32)

        def body(s, carry):
            vbuf[s % RING, s // RING] = vin[pl.ds(SEG * s, 8), :]
            return carry

        lax.fori_loop(0, 128, body, 0)

    v_copy = {}

    def v_first():
        for d in range(1, RING):
            to = (t + d) % RING
            v_copy[d] = remote(vbuf.at[to], va.at[d - 1], va_send.at[d - 1], va_recv.at[d - 1], (f, to))

    def v_second():
        for d in range(1, RING):
            v_copy[d].wait_recv()

        def body(i, carry):
            rows = pl.ds(i * 8, 8)
            vs[rows] = vbuf[t, rows] + va[0, rows] + va[1, rows] + va[2, rows]
            return carry

        lax.fori_loop(0, 4, body, 0)

        def send(d, carry):
            to = (f + d) % 32
            pltpu.make_async_remote_copy(
                src_ref=vs.at[to], dst_ref=vb.at[d - 1], send_sem=vb_send.at[d - 1], recv_sem=vb_recv.at[d - 1],
                device_id=(to, t), device_id_type=MESH,
            ).start()
            return carry

        lax.fori_loop(1, 32, send, 0)

    def v_last():
        def arrive(d, carry):
            pltpu.make_async_remote_copy(
                src_ref=vs.at[f], dst_ref=vb.at[d - 1], send_sem=vb_send.at[d - 1], recv_sem=vb_recv.at[d - 1],
                device_id=((f + d) % 32, t), device_id_type=MESH,
            ).wait()
            return carry

        lax.fori_loop(1, 32, arrive, 0)
        vsum_out[...] = lax.fori_loop(0, 31, lambda d, acc: acc + vb[d], vs[f])

    NT = (((1,), (1,)), ((), ()))
    BLOCK = 256

    def gram_piece(src, add):
        def body(r, carry):
            rows = pl.ds(pl.multiple_of(r * BLOCK, BLOCK), BLOCK)
            d = lax.dot_general(src[rows, :], src[...], NT, preferred_element_type=F32)
            if add:
                d += gram[rows, :]
            gram[rows, :] = d
            return carry

        lax.fori_loop(0, FULL // BLOCK, body, 0)

    def gram_a(src):
        def body(r, carry):
            rows = pl.ds(pl.multiple_of(r * BLOCK, BLOCK), BLOCK)
            am[rows, :] = lax.dot_general(src[rows, :], src[...], NT, preferred_element_type=F32).astype(BF)
            return carry

        lax.fori_loop(0, FULL // BLOCK, body, 0)

    def to_a(scale):
        def body(r, carry):
            rows = pl.ds(pl.multiple_of(r * HALF, HALF), HALF)
            am[rows, :] = (gram[rows, :] * scale).astype(BF) if scale is not None else gram[rows, :].astype(BF)
            return carry

        lax.fori_loop(0, FULL // HALF, body, 0)

    def poly():
        def body(r, carry):
            rows = pl.ds(pl.multiple_of(r * BLOCK, BLOCK), BLOCK)
            block = am[rows, :]
            square = jnp.dot(block, am[...], preferred_element_type=F32)
            bm[rows, :] = (COEF_B * block.astype(F32) + COEF_C * square).astype(BF)
            return carry

        lax.fori_loop(0, FULL // BLOCK, body, 0)

    def advance(src, dst, scale, p=None):
        cols = slice(None) if p is None else pl.ds(AT[p], WIDE[p])
        def body(r, carry):
            rows = pl.ds(pl.multiple_of(r * BLOCK, BLOCK), BLOCK)
            d = jnp.dot(bm[rows, :], src[...], preferred_element_type=F32)
            d = COEF_A * src[rows, :].astype(F32) + d
            dst[rows, cols] = (d * scale).astype(BF) if scale is not None else d.astype(BF)
            return carry

        lax.fori_loop(0, FULL // BLOCK, body, 0)

    exchange(0)
    transit(0)
    load(1)
    exchange(1)
    direct(0)
    load(2)
    exchange(2)
    v_split()
    held = find_owned()
    transit(1)
    v_first()
    second(0)
    direct(1)
    presum(0)
    line(0)
    transit(2)
    second(1)
    line_second(0)
    direct(2)
    presum(1)
    v_second()
    line(1)
    finish(0)
    y_start(0)
    second(2)
    line_second(1)
    y_forward(0)
    presum(2)
    line(2)
    finish(1)
    y_start(1)
    line_second(2)
    gather_step(0, 0)
    y_wait(0)
    finish(2)
    y_start(2)
    y_forward(1)
    gather_step(1, 0)
    gather_step(0, 1)
    gather_step(0, 2)
    gram_piece(xm[0], False)
    y_forward(2)
    gather_step(1, 1)
    gather_step(1, 2)
    share(0)
    v_last()
    y_wait(1)
    share(1)
    gram_piece(xm[1], True)
    y_wait(2)
    gram_piece(xm[2], True)
    share(2)

    def trace(r, acc):
        rows = pl.ds(pl.multiple_of(r * HALF, HALF), HALF)
        ri = lax.broadcasted_iota(jnp.int32, (HALF, FULL), 0) + r * HALF
        ci = lax.broadcasted_iota(jnp.int32, (HALF, FULL), 1)
        return acc + jnp.sum(jnp.where(ri == ci, gram[rows, :], 0.0), axis=0, keepdims=True)

    ss = jnp.sum(lax.fori_loop(0, FULL // HALF, trace, jnp.zeros((1, FULL), F32)), axis=1, keepdims=True)
    scale = 1.5 / (1.5 * jnp.sqrt(ss) + EPS_NORM)
    to_a(scale * scale)
    pick_first(held, 0)
    poly()
    pick_first(held, 1)
    for p in range(PIECES):
        advance(xm[p], xa, scale, p)
    pick_first(held, 2)
    pick_second(held, 0)
    gram_a(xa)
    poly()
    pick_second(held, 1)
    advance(xa, xb, None)
    gram_a(xb)
    pick_second(held, 2)
    mine = pl.ds(my_rows, ROWS)
    block = am[mine, :]
    square = jnp.dot(block, am[...], preferred_element_type=F32)
    last = (COEF_B * block.astype(F32) + COEF_C * square).astype(BF)
    out = jnp.dot(last, xb[...], preferred_element_type=F32)
    ortho = (COEF_A * xb[mine, :].astype(F32) + out).astype(BF)
    upd = 0.2 * math.sqrt(WIDTH) * ortho.astype(F32)
    for b in range(WIDTH // 128):
        ub[pl.ds(b * 128, 128), :] = upd[:, b * 128 : (b + 1) * 128].T

    def pack(d, carry):
        us[d] = ub[pl.ds(pl.multiple_of(d * OUT_COLS, 8), OUT_COLS), :].astype(BF)
        return carry

    lax.fori_loop(0, 32, pack, 0)

    def give_columns(d):
        to = (f + d) % 32
        return pltpu.make_async_remote_copy(
            src_ref=us.at[to], dst_ref=ur.at[f], send_sem=ut_send.at[d - 1], recv_sem=ut_recv.at[d - 1],
            device_id=(to, t), device_id_type=MESH,
        )

    def send(d, carry):
        give_columns(d).start()
        return carry

    lax.fori_loop(1, 32, send, 0)
    stay = pltpu.make_async_copy(us.at[f], ur.at[f], stay_sem)
    stay.start()
    stay.wait()

    for p in range(PIECES):
        pick_last(held, p)

    def take(d, carry):
        give_columns(d).wait()
        return carry

    lax.fori_loop(1, 32, take, 0)
    upd_out[...] = ur[...]
    for copy in waits:
        copy.wait_send()


def dma(*shape):
    return pltpu.SemaphoreType.DMA(shape)


def move(grads, momentum, owners, vec):
    units = (PIECES, 2, RING, 2)
    sends = (PIECES, 2, 6)

    def each(*shape):
        return [pltpu.VMEM((*shape, w), BF) for w in WIDE]

    scratch = [
        each(2, RING, 2, RING, QUARTER),
        each(2, RING, 2, RING, QUARTER),
        each(2, 6, RING, QUARTER),
        each(2, 6, QUARTER),
        each(2, 2, RING, QUARTER),
        each(2, 2, QUARTER),
        each(ROWS),
        pltpu.VMEM((2, ROWS, WIDTH), F32),
        [[pltpu.VMEM((4, QUARTER, w), BF)] * 4 for w in WIDE],
        [[pltpu.VMEM((2, RING, HALF, w), BF)] * 2 for w in WIDE],
        each(2, 6, 2, QUARTER),
        each(2, 6, 2, QUARTER),
        each(FULL),
        pltpu.VMEM((FULL, WIDTH), BF),
        pltpu.VMEM((FULL, WIDTH), BF),
        pltpu.VMEM((FULL, FULL), F32),
        pltpu.VMEM((FULL, FULL), BF),
        pltpu.VMEM((FULL, FULL), BF),
        pltpu.VMEM((WIDTH, ROWS), F32),
        pltpu.VMEM((32, OUT_COLS, ROWS), BF),
        pltpu.VMEM((32, OUT_COLS, ROWS), BF),
        pltpu.VMEM((648, 128), F32),
        pltpu.VMEM((RING, 32, 8, 128), F32),
        pltpu.VMEM((3, 32, 8, 128), F32),
        pltpu.VMEM((32, 8, 128), F32),
        pltpu.VMEM((31, 8, 128), F32),
        pltpu.SMEM((32,), jnp.int32),
        pltpu.SMEM((32,), F32),
        dma(*units), dma(*units), dma(*units),
        pltpu.SemaphoreType.DMA, dma(PIECES, 2, 2), dma(PIECES, 2, 2),
        dma(*sends), dma(*sends), dma(*sends), dma(*sends),
        dma(PIECES, 2, 2), dma(PIECES, 2, 2), dma(PIECES, 2), dma(PIECES, 2),
        dma(2, PIECES, 2, 2), dma(2, PIECES, 2, 2), dma(PIECES, 2), dma(PIECES, 2), dma(*sends), dma(*sends), dma(31), dma(31),
        dma(PIECES, 2), pltpu.SemaphoreType.DMA, pltpu.SemaphoreType.DMA, dma(3), dma(3), dma(31), dma(31),
    ]
    any_space = pl.BlockSpec(memory_space=pl.ANY)
    vmem = pl.BlockSpec(memory_space=pltpu.VMEM)
    return pl.pallas_call(
        kernel,
        out_shape=(
            jax.ShapeDtypeStruct((32, OUT_COLS, ROWS), BF),
            jax.ShapeDtypeStruct((2, ROWS, WIDTH), F32),
            jax.ShapeDtypeStruct((8, 128), F32),
        ),
        in_specs=[any_space, any_space, pl.BlockSpec(memory_space=pltpu.SMEM), any_space],
        out_specs=(vmem, vmem, vmem),
        scratch_shapes=scratch,
        compiler_params=pltpu.CompilerParams(
            collective_id=0, has_side_effects=True, vmem_limit_bytes=63_000_000
        ),
    )(grads, momentum, owners, vec)


def local(grads, momentum, weights, owners, vec_grads, vec_params, vec_m, vec_v):
    update_t, new_momentum, vec_tile = move(
        grads.reshape(RING, RING, 2, ROWS, WIDTH), momentum, owners, vec_grads.reshape(640, 128)
    )
    update = jnp.swapaxes(update_t, 1, 2)
    new_weights = weights * (1.0 - MUON_RATE * DECAY) - MUON_RATE * update.astype(F32)
    vec_sum = vec_tile[:SEG].reshape(SEG * 128)
    new_vec_m = ADAM_ONE * vec_m + (1.0 - ADAM_ONE) * vec_sum
    new_vec_v = ADAM_TWO * vec_v + (1.0 - ADAM_TWO) * vec_sum * vec_sum
    ratio = new_vec_m / BIAS_ONE / (jnp.sqrt(new_vec_v / BIAS_TWO) + ADAM_EPS)
    new_vec_params = vec_params - VEC_RATE * (ratio + DECAY * vec_params)
    return (new_weights, update, new_momentum, new_vec_params, new_vec_m, new_vec_v)


def solution(mesh):
    placed = (
        P("fsdp", None, "tp", None),
        P("fsdp", "tp", None),
        P(None, "tp", "fsdp"),
        P(),
        P(("fsdp", "tp"), None),
        P(("fsdp", "tp")),
        P(("fsdp", "tp")),
        P(("fsdp", "tp")),
    )
    return jax.shard_map(
        local,
        mesh=mesh,
        in_specs=placed,
        out_specs=(
            P(None, "tp", "fsdp"),
            P(None, "tp", "fsdp"),
            P("fsdp", "tp", None),
            P(("fsdp", "tp")),
            P(("fsdp", "tp")),
            P(("fsdp", "tp")),
        ),
        check_vma=False,
    )
```
